32 devices in a mesh: dp: 8 (over y, x, core), seq: 4 (over z).
Axes of the slice: x: 2, y: 2, z: 4, core: 2. Of those that a mesh axis runs over, the one named last changes fastest.
Arguments:
- tokens: bfloat16 [2, 8, 2048, 768], P(None, 'dp', 'seq'), may hold values from -6 to 6
- seq_lengths: int32 [2, 8], P(None, 'dp'), may hold values from 512 to 2048, as said below
- query_weight: bfloat16 [768, 768], P(('dp', 'seq')), may hold values from -0.21875 to 0.21875
- query_bias: bfloat16 [768], P(('dp', 'seq')), may hold values from -3 to 3
- key_weight: bfloat16 [768, 768], P(('dp', 'seq')), may hold values from -0.21875 to 0.21875
- key_bias: bfloat16 [768], P(('dp', 'seq')), may hold values from -3 to 3
- value_weight: bfloat16 [768, 768], P(('dp', 'seq')), may hold values from -0.21875 to 0.21875
- value_bias: bfloat16 [768], P(('dp', 'seq')), may hold values from -3 to 3
- output_weight: bfloat16 [768, 768], P(('dp', 'seq')), may hold values from -1.25 to 1.25
- output_bias: bfloat16 [768], P(('dp', 'seq')), may hold values from -3 to 3
- gain_first: bfloat16 [768], P(('dp', 'seq')), may hold values from 0.5 to 1.5
- shift_first: bfloat16 [768], P(('dp', 'seq')), may hold values from -3 to 3
- inner_weight: bfloat16 [768, 3072], P(('dp', 'seq')), may hold values from -0.21875 to 0.21875
- inner_bias: bfloat16 [3072], P(('dp', 'seq')), may hold values from -3 to 3
- outer_weight: bfloat16 [3072, 768], P(('dp', 'seq')), may hold values from -0.109375 to 0.109375
- outer_bias: bfloat16 [768], P(('dp', 'seq')), may hold values from -3 to 3
- gain_second: bfloat16 [768], P(('dp', 'seq')), may hold values from 0.5 to 1.5
- shift_second: bfloat16 [768], P(('dp', 'seq')), may hold values from -3 to 3
- cotangent: bfloat16 [2, 8, 2048, 768], P(None, 'dp', 'seq'), may hold values from -6 to 6
Outputs:
- layer_out: bfloat16 [2, 8, 2048, 768], P(None, 'dp', 'seq')
- grad_tokens: float32 [2, 8, 2048, 768], P(None, 'dp', 'seq')
- grad_query_weight: float32 [768, 768], P(('dp', 'seq'))
- grad_query_bias: float32 [768], P(('dp', 'seq'))
- grad_key_weight: float32 [768, 768], P(('dp', 'seq'))
- grad_key_bias: float32 [768], P(('dp', 'seq'))
- grad_value_weight: float32 [768, 768], P(('dp', 'seq'))
- grad_value_bias: float32 [768], P(('dp', 'seq'))
- grad_output_weight: float32 [768, 768], P(('dp', 'seq'))
- grad_output_bias: float32 [768], P(('dp', 'seq'))
- grad_gain_first: float32 [768], P(('dp', 'seq'))
- grad_shift_first: float32 [768], P(('dp', 'seq'))
- grad_inner_weight: float32 [768, 3072], P(('dp', 'seq'))
- grad_inner_bias: float32 [3072], P(('dp', 'seq'))
- grad_outer_weight: float32 [3072, 768], P(('dp', 'seq'))
- grad_outer_bias: float32 [768], P(('dp', 'seq'))
- grad_gain_second: float32 [768], P(('dp', 'seq'))
- grad_shift_second: float32 [768], P(('dp', 'seq'))
The draws below stay inside these ranges and needn't reach their ends.
Inputs may be any that keep to these rules, and one draw needn't show every extreme that they name: `seq_lengths`: in every micro-batch some sequence has exactly 2048 valid positions; positions at or past a sequence's length are padding.
All inputs are finite; a program needn't handle non-finite values.
Results may differ from the reference program's by a relative error of at most 0.014.
Values may be sent and summed in bfloat16 or wider, within the bound.
No kernel may reach another device: no remote copies, remote signals or barrier semaphores. Data moves between devices by JAX's collectives and lax.ppermute only.
A program may use at most 192 MiB of HBM per device.

```python
import math
import jax
import jax.numpy as jnp
from jax import lax

D = 768
H = 12
HD = 64
FF = 3072
LEN = 2048
BLOCK = 512
MB = 2
SEQS = 1
NSEQ = 8
N_DP = 8


def draw_seq_lengths(key, part):
    key_length, key_longest = jax.random.split(jax.random.fold_in(key, 7))
    lengths_drawn = jax.random.randint(key_length, (MB, NSEQ), LEN // 4, LEN + 1)
    longest = jax.random.randint(key_longest, (MB,), 0, NSEQ)
    column = jnp.arange(NSEQ)[None, :]
    return jnp.where(column == longest[:, None], LEN, lengths_drawn).astype(jnp.int32)


def level_of(rng, dims, cuts, low, top_value):
    factor_of, own = 1.0, jax.random.fold_in(rng, 6)
    for axis_at, parts in cuts:
        heights = jnp.exp(jax.random.uniform(jax.random.fold_in(own, axis_at), (parts,), jnp.float32, low / len(cuts), top_value / len(cuts)))
        factor_of = factor_of * jnp.repeat(heights, dims[axis_at] // parts).reshape([-1 if axis == axis_at else 1 for axis in range(len(dims))])
    return factor_of


def bell_draw(key, extent, deviation, most, cuts=(), held_as=jnp.bfloat16):
    values = deviation * jax.random.normal(key, extent, jnp.float32)
    if cuts:
        values = values * level_of(key, extent, cuts, -0.22, 0.18)
    return jnp.clip(values, -most, most).astype(held_as)


def setup_inputs(seed: int = 0) -> dict:
    keys = jax.random.split(jax.random.key(seed), 20)
    tokens = bell_draw(keys[0], (MB, NSEQ, LEN, D), 1.0, 6.0, ((1, 8), (2, 4)))
    seq_lengths = draw_seq_lengths(jax.random.fold_in(keys[19], 71), 0)
    query_weight = bell_draw(keys[2], (D, D), D ** -0.5, 0.21875, ((0, 32),))
    query_bias = bell_draw(keys[3], (D,), 0.5, 3.0, ((0, 32),))
    key_weight = bell_draw(keys[4], (D, D), D ** -0.5, 0.21875, ((0, 32),))
    key_bias = bell_draw(keys[5], (D,), 0.5, 3.0, ((0, 32),))
    value_weight = bell_draw(keys[6], (D, D), D ** -0.5, 0.21875, ((0, 32),))
    value_bias = bell_draw(keys[7], (D,), 0.5, 3.0, ((0, 32),))
    output_weight = bell_draw(keys[8], (D, D), (D // 32) ** -0.5, 1.25, ((0, 32),))
    output_bias = bell_draw(keys[9], (D,), 0.5, 3.0, ((0, 32),))
    gain_first = jnp.clip(1.0 + 0.1 * jax.random.normal(keys[10], (D,), jnp.float32), 0.5, 1.5).astype(jnp.bfloat16)
    shift_first = bell_draw(keys[11], (D,), 0.5, 3.0, ((0, 32),))
    inner_weight = bell_draw(keys[12], (D, FF), D ** -0.5, 0.21875, ((0, 32),))
    inner_bias = bell_draw(keys[13], (FF,), 0.5, 3.0, ((0, 32),))
    outer_weight = bell_draw(keys[14], (FF, D), FF ** -0.5, 0.109375, ((0, 32),))
    outer_bias = bell_draw(keys[15], (D,), 0.5, 3.0, ((0, 32),))
    gain_second = jnp.clip(1.0 + 0.1 * jax.random.normal(keys[16], (D,), jnp.float32), 0.5, 1.5).astype(jnp.bfloat16)
    shift_second = bell_draw(keys[17], (D,), 0.5, 3.0, ((0, 32),))
    cotangent = bell_draw(keys[18], (MB, NSEQ, LEN, D), 1.0, 6.0, ((1, 8), (2, 4)))
    return dict(tokens=tokens, seq_lengths=seq_lengths, query_weight=query_weight, query_bias=query_bias, key_weight=key_weight, key_bias=key_bias, value_weight=value_weight, value_bias=value_bias, output_weight=output_weight, output_bias=output_bias, gain_first=gain_first, shift_first=shift_first, inner_weight=inner_weight, inner_bias=inner_bias, outer_weight=outer_weight, outer_bias=outer_bias, gain_second=gain_second, shift_second=shift_second, cotangent=cotangent)


@jax.custom_vjp
def low(v):
    return lax.optimization_barrier(v.astype(jnp.bfloat16)).astype(jnp.float32)

@jax.custom_vjp
def low_back(v):
    return v

def low_keep(v):
    return (low(v), None)

def low_pass(kept, grad):
    return (grad,)

def back_keep(v):
    return (v, None)

def back_low(kept, grad):
    return (low(grad),)
low.defvjp(low_keep, low_pass)
low_back.defvjp(back_keep, back_low)
NORM_EPS = 1e-05
HALF_TURN = math.pi / 2

def matmul(left_side, right_side):
    return jnp.dot(left_side, right_side, precision=lax.Precision.HIGHEST)

def layer_norm(values, norm_gain, norm_shift):
    center = values - lax.optimization_barrier(jnp.mean(values, axis=-1, keepdims=True))
    spread = lax.optimization_barrier(jnp.mean(center * center, axis=-1, keepdims=True))
    return center * lax.rsqrt(spread + NORM_EPS) * norm_gain + norm_shift

def reweight(places, limit):
    angle = HALF_TURN * places[:, None] / limit[None, :]
    live = (places[:, None] < limit[None, :]).astype(jnp.float32)
    return (jnp.cos(angle) * live, jnp.sin(angle) * live)

def attention(queries, key_rows, values, lengths, offset, initial):
    total_rows, head_count, head_size = queries.shape
    block_rows = min(BLOCK, total_rows)
    block_count = total_rows // block_rows
    limit = lengths.astype(jnp.float32)
    causal = jnp.tril(jnp.ones((block_rows, block_rows), jnp.float32))
    highest = lax.Precision.HIGHEST

    def attend(state_now, inputs):
        sum_cos, sum_sin, norm_cos, norm_sin = state_now
        query_blk, key_blk, value_blk, block_index = inputs
        places = (offset + block_index * block_rows + jnp.arange(block_rows)).astype(jnp.float32)
        weight_cos, weight_sin = reweight(places, limit)
        query_relu = jax.nn.relu(query_blk)
        key_relu = jax.nn.relu(key_blk)
        query_cos = query_relu * weight_cos[:, :, None]
        query_sin = query_relu * weight_sin[:, :, None]
        key_cos = key_relu * weight_cos[:, :, None]
        key_sin = key_relu * weight_sin[:, :, None]
        scores = jnp.einsum('igd,jgd->gij', query_cos, key_cos, precision=highest)
        scores = scores + jnp.einsum('igd,jgd->gij', query_sin, key_sin, precision=highest)
        scores = scores * causal[None, :, :]
        numer = jnp.einsum('gij,jge->ige', scores, value_blk, precision=highest)
        numer = numer + jnp.einsum('igd,gde->ige', query_cos, sum_cos, precision=highest)
        numer = numer + jnp.einsum('igd,gde->ige', query_sin, sum_sin, precision=highest)
        denom = lax.optimization_barrier(jnp.sum(scores, axis=2)).T
        denom = denom + jnp.einsum('igd,gd->ig', query_cos, norm_cos, precision=highest)
        denom = denom + jnp.einsum('igd,gd->ig', query_sin, norm_sin, precision=highest)
        output = numer / jnp.maximum(denom, 1.0)[:, :, None]
        sum_cos = sum_cos + jnp.einsum('jgd,jge->gde', key_cos, value_blk, precision=highest)
        sum_sin = sum_sin + jnp.einsum('jgd,jge->gde', key_sin, value_blk, precision=highest)
        norm_cos = norm_cos + lax.optimization_barrier(jnp.sum(key_cos, axis=0))
        norm_sin = norm_sin + lax.optimization_barrier(jnp.sum(key_sin, axis=0))
        return ((sum_cos, sum_sin, norm_cos, norm_sin), output)
    stacked = (queries.reshape(block_count, block_rows, head_count, head_size), key_rows.reshape(block_count, block_rows, head_count, head_size), values.reshape(block_count, block_rows, head_count, head_size), jnp.arange(block_count))
    final_state, outputs = lax.scan(jax.checkpoint(attend), initial, stacked)
    return outputs.reshape(total_rows, head_count, head_size)

def to_heads(array):
    return array.reshape(SEQS, LEN, H, HD).transpose(1, 0, 2, 3).reshape(LEN, SEQS * H, HD)

def forward(weights, rows_in, lengths):
    w_query, b_query, w_key, b_key, w_value, b_value, w_output, b_output, gain_one, shift_one, w_inner, b_inner, w_outer, b_outer, gain_two, shift_two = weights
    query_full = low(low_back(matmul(rows_in, w_query) + b_query))
    key_full = low(low_back(matmul(rows_in, w_key) + b_key))
    value_full = low(low_back(matmul(rows_in, w_value) + b_value))
    head_lengths = jnp.repeat(lengths, H)
    heads_total = SEQS * H
    initial = (jnp.zeros((heads_total, HD, HD), jnp.float32), jnp.zeros((heads_total, HD, HD), jnp.float32), jnp.zeros((heads_total, HD), jnp.float32), jnp.zeros((heads_total, HD), jnp.float32))
    mixed_heads = attention(to_heads(query_full), to_heads(key_full), to_heads(value_full), head_lengths, 0, initial)
    mixed = mixed_heads.reshape(LEN, SEQS, D).transpose(1, 0, 2)
    mixed = low(low_back(mixed))
    attended = low_back(matmul(mixed, w_output) + b_output)
    first = layer_norm(rows_in + attended, gain_one, shift_one)
    inner = low_back(matmul(low(first), w_inner) + b_inner)
    hidden = low(jax.nn.gelu(inner))
    outer = low_back(matmul(hidden, w_outer) + b_outer)
    return layer_norm(first + outer, gain_two, shift_two)

def reference(tokens, seq_lengths, query_weight, query_bias, key_weight, key_bias, value_weight, value_bias, output_weight, output_bias, gain_first, shift_first, inner_weight, inner_bias, outer_weight, outer_bias, gain_second, shift_second, cotangent):
    params = tuple((weight_item.astype(jnp.float32) for weight_item in (query_weight, query_bias, key_weight, key_bias, value_weight, value_bias, output_weight, output_bias, gain_first, shift_first, inner_weight, inner_bias, outer_weight, outer_bias, gain_second, shift_second)))
    group_count = MB * N_DP
    token_groups = tokens.astype(jnp.float32).reshape(group_count, SEQS, LEN, D)
    length_groups = seq_lengths.astype(jnp.int32).reshape(group_count, SEQS)
    cot_groups = cotangent.astype(jnp.float32).reshape(group_count, SEQS, LEN, D)
    zero_grads = jax.tree.map(jnp.zeros_like, params)

    def one_group(totals, inputs):
        group_tokens, group_lengths, group_cot = inputs

        def group_forward(weights, rows_in):
            return forward(weights, rows_in, group_lengths)
        result, pullback = jax.vjp(group_forward, params, group_tokens)
        grad_weights, grad_rows = pullback(group_cot)
        totals = jax.tree.map(jnp.add, totals, grad_weights)
        return (totals, (result.astype(jnp.bfloat16), grad_rows))
    totals, (out_groups, grad_groups) = lax.scan(one_group, zero_grads, (token_groups, length_groups, cot_groups))
    layer_out = out_groups.reshape(MB, NSEQ, LEN, D)
    grad_tokens = grad_groups.reshape(MB, NSEQ, LEN, D)
    return (layer_out, grad_tokens, totals[0], totals[1], totals[2], totals[3], totals[4], totals[5], totals[6], totals[7], totals[8], totals[9], totals[10], totals[11], totals[12], totals[13], totals[14], totals[15])
```

```python
import math

import jax
import jax.numpy as jnp
from jax import lax
from jax.experimental import pallas as pl
from jax.experimental.pallas import tpu as pltpu
from jax.sharding import PartitionSpec as P

H = 12
HD = 64
LANES = 128
NORM_EPS = 1e-05
HALF_TURN = math.pi / 2
STATE_ROWS = 72
GELU_A = 0.7978845608028654
GELU_B = 0.044715
BF = jnp.bfloat16
F32 = jnp.float32


def dot_nn(a, b):
    return lax.dot_general(a, b, (((1,), (0,)), ((), ())), preferred_element_type=F32)


def dot_nt(a, b):
    return lax.dot_general(a, b, (((1,), (1,)), ((), ())), preferred_element_type=F32)


def dot_tn(a, b):
    return lax.dot_general(a, b, (((0,), (0,)), ((), ())), preferred_element_type=F32)


def lane_first(shape):
    return lax.broadcasted_iota(jnp.int32, shape, 1) < HD


def pair_ones():
    row = lax.broadcasted_iota(jnp.int32, (LANES, LANES), 0) < HD
    col = lax.broadcasted_iota(jnp.int32, (LANES, LANES), 1) < HD
    return (row == col).astype(F32)


def head_sum(values, ones_low):
    high = values.astype(BF)
    rest = (values - high.astype(F32)).astype(BF)
    return dot_nn(jnp.concatenate([high, rest], axis=1), jnp.concatenate([ones_low, ones_low], axis=0))


def spread_state(packed):
    first = lane_first((HD, LANES))
    zero = jnp.zeros_like(packed)
    return jnp.concatenate(
        [jnp.where(first, packed, zero), jnp.where(first, zero, packed)], axis=0
    ).astype(BF)


def pack_state(full, row):
    first = lane_first((HD, LANES))
    packed = jnp.where(first, full[:HD], full[HD:])
    tail = jnp.concatenate([row, jnp.zeros((STATE_ROWS - HD - 1, LANES), F32)], axis=0)
    return jnp.concatenate([packed, tail], axis=0)


def key_state_kernel(k_ref, v_ref, cos_ref, sin_ref, out_ref):
    keys = jnp.maximum(k_ref[...], 0)
    vals = v_ref[...].astype(F32)
    cos, sin = cos_ref[...], sin_ref[...]
    both = jnp.concatenate([(vals * cos).astype(BF), (vals * sin).astype(BF)], axis=1)
    full = dot_tn(keys, both)
    keys32 = keys.astype(F32)
    row_cos = jnp.sum(keys32 * cos, axis=0, keepdims=True)
    row_sin = jnp.sum(keys32 * sin, axis=0, keepdims=True)
    out_ref[0, 0] = pack_state(full[:, :LANES], row_cos).astype(BF)
    out_ref[0, 1] = pack_state(full[:, LANES:], row_sin).astype(BF)


def tile_rows(rows):
    return min(256, rows)


def mix_kernel(q_ref, k_ref, v_ref, b_ref, w_ref, cos_ref, sin_ref, st_ref, mixed_ref, out_ref, den_ref):
    rows = q_ref.shape[0]
    tile = tile_rows(rows)
    ones_pair = pair_ones().astype(BF)
    keys = jnp.maximum(k_ref[...], 0)
    vals = jnp.concatenate([v_ref[...], jnp.ones((rows, LANES), BF)], axis=1)
    states = jnp.concatenate(
        [spread_state(st_ref[0, 0, :HD]), spread_state(st_ref[0, 1, :HD])], axis=1
    )
    row_cos, row_sin = st_ref[0, 0, HD : HD + 1], st_ref[0, 1, HD : HD + 1]
    first = lane_first((tile, LANES))
    for step in range(rows // tile):
        at = slice(step * tile, (step + 1) * tile)
        seen = (step + 1) * tile
        query = jnp.maximum(q_ref[at], 0)
        cos, sin = cos_ref[at], sin_ref[at]
        zero = jnp.zeros_like(query)
        weight = w_ref[0, at, :seen]
        heads = []
        for own in (jnp.where(first, query, zero), jnp.where(first, zero, query)):
            scores = dot_nt(own, keys[:seen]) * weight
            heads.append(dot_nn(scores.astype(BF), vals[:seen]))
        num = jnp.where(first, heads[0][:, :LANES], heads[1][:, :LANES])
        den = jnp.where(first, heads[0][:, LANES:], heads[1][:, LANES:])
        past = dot_nn(query, states)
        num = num + cos * past[:, :LANES] + sin * past[:, LANES:]
        den = den + head_sum(query.astype(F32) * (cos * row_cos + sin * row_sin), ones_pair)
        out = (num + den * b_ref[...]) / jnp.maximum(den, 1.0)
        mixed_ref[at] = out.astype(BF)
        out_ref[at] = out
        den_ref[at] = den


def mix_grads(d_out, out, den, bias, ones_pair):
    inverse = 1.0 / jnp.maximum(den, 1.0)
    d_num = (d_out.astype(F32) * inverse).astype(BF)
    gate = jnp.where(den > 1.0, 1.0, jnp.where(den == 1.0, 0.5, 0.0))
    return d_num, head_sum(d_num.astype(F32) * (bias - out * gate), ones_pair)


def query_state_kernel(q_ref, d_ref, out_ref, den_ref, b_ref, cos_ref, sin_ref, st_ref):
    ones_pair = pair_ones().astype(BF)
    query = jnp.maximum(q_ref[...], 0)
    cos, sin = cos_ref[...], sin_ref[...]
    d_num, d_den = mix_grads(d_ref[...], out_ref[...], den_ref[...], b_ref[...], ones_pair)
    d_num32 = d_num.astype(F32)
    both = jnp.concatenate([(d_num32 * cos).astype(BF), (d_num32 * sin).astype(BF)], axis=1)
    full = dot_tn(query, both)
    part = query.astype(F32) * d_den
    st_ref[0, 0] = pack_state(full[:, :LANES], jnp.sum(part * cos, axis=0, keepdims=True)).astype(BF)
    st_ref[0, 1] = pack_state(full[:, LANES:], jnp.sum(part * sin, axis=0, keepdims=True)).astype(BF)


def mix_back_kernel(
    q_ref, k_ref, v_ref, d_ref, out_ref, den_ref, b_ref, low_ref, up_ref, cos_ref, sin_ref, past_ref, next_ref,
    dq_ref, dk_ref, dv_ref,
):
    rows = q_ref.shape[0]
    tile = tile_rows(rows)
    ones_pair = pair_ones().astype(BF)
    first = lane_first((rows, LANES))
    lane = lax.broadcasted_iota(jnp.int32, (rows, LANES), 1)
    query = jnp.maximum(q_ref[...], 0)
    keys = jnp.maximum(k_ref[...], 0)
    vals = v_ref[...]
    cos, sin = cos_ref[...], sin_ref[...]
    d_num, d_den = mix_grads(d_ref[...], out_ref[...], den_ref[...], b_ref[...], ones_pair)
    high = d_den.astype(BF)
    rest = (d_den - high.astype(F32)).astype(BF)
    zero = jnp.zeros((rows, LANES), BF)
    spot = lane % HD
    marks = jnp.where(spot == 0, high, jnp.where(spot == 1, rest, zero))
    vals_one = jnp.concatenate([vals, jnp.ones((rows, LANES), BF)], axis=1)

    past = [spread_state(past_ref[0, i, :HD]) for i in range(2)]
    past_row = [past_ref[0, i, HD : HD + 1] for i in range(2)]
    d_query = cos * dot_nt(d_num, past[0]) + sin * dot_nt(d_num, past[1])
    d_query = d_query + d_den * (cos * past_row[0] + sin * past_row[1])
    later = [spread_state(next_ref[0, i, :HD]) for i in range(2)]
    later_row = [next_ref[0, i, HD : HD + 1] for i in range(2)]
    d_keys = cos * (dot_nt(vals, later[0]) + later_row[0]) + sin * (dot_nt(vals, later[1]) + later_row[1])
    from_keys = dot_nn(keys, jnp.concatenate(later, axis=1))
    d_vals = cos * from_keys[:, :LANES] + sin * from_keys[:, LANES:]

    own_query = (jnp.where(first, query, zero), jnp.where(first, zero, query))
    own_d = tuple(
        jnp.concatenate([jnp.where(pick, d_num, zero), jnp.where(pick, marks, zero)], axis=1)
        for pick in (first, jnp.logical_not(first))
    )
    for step in range(rows // tile):
        at = slice(step * tile, (step + 1) * tile)
        seen = (step + 1) * tile
        some = first[at]
        parts = []
        for one in range(2):
            d_scores = dot_nt(own_d[one][at], vals_one[:seen]) * low_ref[0, at, :seen]
            parts.append(dot_nn(d_scores.astype(BF), keys[:seen]))
        total = d_query[at] + jnp.where(some, parts[0], parts[1])
        dq_ref[at] = jnp.where(q_ref[at] > 0, total, 0.0).astype(BF)
        onward = slice(step * tile, rows)
        weight = up_ref[0, at, onward]
        key_parts, val_parts = [], []
        for one in range(2):
            scores = dot_nt(keys[at], own_query[one][onward]) * weight
            val_parts.append(dot_nn(scores.astype(BF), d_num[onward]))
            d_scores = dot_nt(vals_one[at], own_d[one][onward]) * weight
            key_parts.append(dot_nn(d_scores.astype(BF), query[onward]))
        total = d_keys[at] + jnp.where(some, key_parts[0], key_parts[1])
        dk_ref[at] = jnp.where(k_ref[at] > 0, total, 0.0).astype(BF)
        dv_ref[at] = (d_vals[at] + jnp.where(some, val_parts[0], val_parts[1])).astype(BF)


class Mixer:
    def __init__(self, count, rows, width):
        self.count, self.rows, self.width = count, rows, width
        self.pairs = width // LANES

    def wide(self, group=0):
        offset = group * self.pairs
        return pl.BlockSpec((self.rows, LANES), lambda m, p: (m, offset + p))

    def angle(self):
        return pl.BlockSpec((self.rows, LANES), lambda m, p: (m, 0))

    def bias(self):
        return pl.BlockSpec((1, LANES), lambda m, p: (0, p))

    def state(self):
        return pl.BlockSpec((1, 2, STATE_ROWS, LANES), lambda m, p: (m, 0, 0, p))

    def square(self):
        return pl.BlockSpec((1, self.rows, self.rows), lambda m, p: (m, 0, 0))

    def state_shape(self):
        return jax.ShapeDtypeStruct((self.count, 2, STATE_ROWS, self.width), BF)

    def flat_shape(self, dtype):
        return jax.ShapeDtypeStruct((self.count * self.rows, self.width), dtype)

    def call(self, kernel, in_specs, out_specs, out_shape, flops):
        return pl.pallas_call(
            kernel,
            grid=(self.count, self.pairs),
            in_specs=in_specs,
            out_specs=out_specs,
            out_shape=out_shape,
            cost_estimate=pl.CostEstimate(
                flops=flops * self.count * self.pairs, bytes_accessed=1 << 23, transcendentals=0
            ),
        )

    def key_states(self, qkv, cos, sin):
        flops = 4 * self.rows * LANES * LANES
        return self.call(
            key_state_kernel,
            [self.wide(1), self.wide(2), self.angle(), self.angle()],
            self.state(),
            self.state_shape(),
            flops,
        )(qkv, qkv, cos, sin)

    def mix(self, qkv, bias, low, cos, sin, past):
        flops = 12 * self.rows * self.rows * LANES
        return self.call(
            mix_kernel,
            [self.wide(0), self.wide(1), self.wide(2), self.bias(), self.square(), self.angle(), self.angle(), self.state()],
            [self.wide()] * 3,
            [self.flat_shape(BF), self.flat_shape(F32), self.flat_shape(F32)],
            flops,
        )(qkv, qkv, qkv, bias, low, cos, sin, past)

    def query_states(self, qkv, d_mixed, out, den, bias, cos, sin):
        flops = 4 * self.rows * LANES * LANES
        return self.call(
            query_state_kernel,
            [self.wide(0)] + [self.wide()] * 3 + [self.bias()] + [self.angle()] * 2,
            self.state(),
            self.state_shape(),
            flops,
        )(qkv, d_mixed, out, den, bias, cos, sin)

    def mix_back(self, qkv, d_mixed, out, den, bias, low, up, cos, sin, past, later):
        flops = 30 * self.rows * self.rows * LANES
        return self.call(
            mix_back_kernel,
            [self.wide(0), self.wide(1), self.wide(2)]
            + [self.wide()] * 3
            + [self.bias()]
            + [self.square()] * 2
            + [self.angle()] * 2
            + [self.state()] * 2,
            [self.wide()] * 3,
            [self.flat_shape(BF)] * 3,
            flops,
        )(qkv, qkv, qkv, d_mixed, out, den, bias, low, up, cos, sin, past, later)


def outside_sum(state, forward):
    size = lax.axis_size("seq")

    def shift(values, distance):
        if forward:
            pairs = [(i, i + distance) for i in range(size - distance)]
        else:
            pairs = [(i + distance, i) for i in range(size - distance)]
        return lax.ppermute(values, "seq", pairs)

    moved = shift(state, 1)
    total = moved.astype(F32)
    reach = 1
    while reach + 1 < size:
        span = min(reach + 1, size - 1 - reach)
        block = (state.astype(F32) + total).astype(BF)
        if span < reach + 1:
            raise NotImplementedError
        got = shift(block, span)
        total = total + got.astype(F32)
        reach = reach + span
    return total


def swap(values, bit):
    size = lax.axis_size("dp")
    return lax.ppermute(values, "dp", [(i, i ^ (1 << bit)) for i in range(size)])


def scatter_sum(pieces):
    dp_size, seq_size, rows, width = pieces.shape
    bits = dp_size.bit_length() - 1
    place = lax.axis_index("dp")

    def fold(values, axis, bit):
        mine = (place >> bit) & 1
        kept = lax.dynamic_index_in_dim(values, mine, axis, keepdims=False)
        sent = lax.dynamic_index_in_dim(values, 1 - mine, axis, keepdims=False)
        return (kept.astype(F32) + swap(sent.astype(BF), bit).astype(F32)).astype(BF)

    values = pieces.reshape((2,) * bits + (seq_size, rows, width))
    values = fold(values, bits - 1, 0)
    half = (bits - 1) // 2
    others = list(range(1, bits))
    orders = (others[:half] + others[half:], others[half:] + others[:half])
    cut = (rows // 2 + 7) // 8 * 8
    z = lax.axis_index("seq")
    results = []
    for order, span in zip(orders, (slice(0, cut), slice(cut, rows))):
        part = values[..., span, :]
        left = list(others)
        for bit in order:
            axis = [b for b in sorted(left, reverse=True)].index(bit)
            part = fold(part, axis, bit)
            left.remove(bit)
        total = lax.dynamic_index_in_dim(part, z, 0, keepdims=False).astype(F32)
        for distance in range(1, seq_size):
            sent = lax.dynamic_index_in_dim(part, (z + distance) % seq_size, 0, keepdims=False)
            got = lax.ppermute(sent, "seq", [(i, (i + distance) % seq_size) for i in range(seq_size)])
            total = total + got.astype(F32)
        results.append(total)
    return jnp.concatenate(results, axis=0)


def norm_stats(values):
    center = values - jnp.mean(values, axis=-1, keepdims=True)
    spread = jnp.mean(center * center, axis=-1, keepdims=True)
    scale = lax.rsqrt(spread + NORM_EPS)
    return center * scale, scale


def norm_back(grad, normed, scale, gain):
    inner = grad * gain
    return scale * (
        inner
        - jnp.mean(inner, axis=-1, keepdims=True)
        - normed * jnp.mean(inner * normed, axis=-1, keepdims=True)
    )


def per_device(
    tokens,
    seq_lengths,
    query_weight,
    query_bias,
    key_weight,
    key_bias,
    value_weight,
    value_bias,
    output_weight,
    output_bias,
    gain_first,
    shift_first,
    inner_weight,
    inner_bias,
    outer_weight,
    outer_bias,
    gain_second,
    shift_second,
    cotangent,
):
    dp_size, seq_size = lax.axis_size("dp"), lax.axis_size("seq")
    owners = dp_size * seq_size
    micro_count, seqs_here, shard_rows, width = tokens.shape
    count = micro_count * seqs_here
    total = count * shard_rows
    share = query_weight.shape[0]
    hidden_width = inner_weight.shape[1]
    fan = hidden_width // width
    seq_place = lax.axis_index("seq")
    mixer = Mixer(count, shard_rows, width)

    vectors = [query_bias, key_bias, value_bias, output_bias, gain_first, shift_first, outer_bias, gain_second, shift_second]
    vector_row = jnp.concatenate(vectors + [inner_bias])
    vector_fill = width - vector_row.shape[0]
    vector_block = jnp.pad(vector_row[None, :], ((0, 7), (0, vector_fill)))
    head_rows = jnp.concatenate([vector_block, query_weight, key_weight, value_weight], axis=0)
    tail_rows = jnp.concatenate(
        [output_weight] + [inner_weight[:, i * width : (i + 1) * width] for i in range(fan)] + [outer_weight], axis=0
    )
    head_all = lax.all_gather(head_rows, ("dp", "seq"), axis=0)
    tail_all = lax.all_gather(tail_rows, ("dp", "seq"), axis=0)

    vec = head_all[:, 0, :].astype(F32)
    (b_query, b_key, b_value, b_output, gain_one, shift_one, b_outer, gain_two, shift_two) = (
        vec[:, i * share : (i + 1) * share].reshape(width) for i in range(9)
    )
    b_inner = vec[:, 9 * share : 9 * share + hidden_width // owners].reshape(hidden_width)
    w_qkv = jnp.concatenate(
        [head_all[:, 8 + i * share : 8 + (i + 1) * share].reshape(width, width) for i in range(3)], axis=1
    )
    b_qkv = jnp.concatenate([b_query, b_key, jnp.zeros((width,), F32)])
    bias_row = b_value[None, :]
    w_output = tail_all[:, :share].reshape(width, width)
    w_inner = jnp.concatenate(
        [tail_all[:, (1 + i) * share : (2 + i) * share].reshape(width, width) for i in range(fan)], axis=1
    )
    w_outer = tail_all[:, (1 + fan) * share :].reshape(hidden_width, width)

    limit = seq_lengths.reshape(count).astype(F32)
    places = (seq_place * shard_rows + jnp.arange(shard_rows)).astype(F32)
    angle = HALF_TURN * places[None, :] / limit[:, None]
    live = (places[None, :] < limit[:, None]).astype(F32)
    cos, sin = jnp.cos(angle) * live, jnp.sin(angle) * live
    square = cos[:, :, None] * cos[:, None, :] + sin[:, :, None] * sin[:, None, :]
    causal = jnp.tril(jnp.ones((shard_rows, shard_rows), F32))
    low, up = square * causal, square * causal.T
    cos = jnp.broadcast_to(cos.reshape(total, 1), (total, LANES))
    sin = jnp.broadcast_to(sin.reshape(total, 1), (total, LANES))

    x_low = tokens.reshape(total, width)
    qkv = (dot_nn(x_low, w_qkv) + b_qkv).astype(BF)
    states = mixer.key_states(qkv, cos, sin)
    past = outside_sum(states, True)
    mixed, mixed_full, den = mixer.mix(qkv, bias_row, low, cos, sin, past)

    resid_one = x_low.astype(F32) + (dot_nn(mixed, w_output) + b_output)
    norm_one, scale_one = norm_stats(resid_one)
    first = norm_one * gain_one + shift_one
    first_low = first.astype(BF)
    inner = dot_nn(first_low, w_inner) + b_inner
    bent = jnp.tanh(GELU_A * (inner + GELU_B * inner * inner * inner))
    hidden = (0.5 * inner * (1.0 + bent)).astype(BF)
    outer = dot_nn(hidden, w_outer) + b_outer
    norm_two, scale_two = norm_stats(first + outer)
    layer_out = (norm_two * gain_two + shift_two).astype(BF)

    grad_final = cotangent.reshape(total, width).astype(F32)
    grad_gain_two = jnp.sum(grad_final * norm_two, axis=0)
    grad_shift_two = jnp.sum(grad_final, axis=0)
    d_second = norm_back(grad_final, norm_two, scale_two, gain_two)
    d_outer = d_second.astype(BF)
    grad_w_outer = dot_tn(hidden, d_outer)
    grad_b_outer = jnp.sum(d_outer.astype(F32), axis=0)
    d_hidden = dot_nt(d_outer, w_outer)
    slope = 0.5 * (1.0 + bent) + 0.5 * inner * (1.0 - bent * bent) * GELU_A * (1.0 + 3.0 * GELU_B * inner * inner)
    d_inner = (d_hidden * slope).astype(BF)
    grad_w_inner = dot_tn(first_low, d_inner)
    grad_b_inner = jnp.sum(d_inner.astype(F32), axis=0)
    d_first = d_second + dot_nt(d_inner, w_inner)
    grad_gain_one = jnp.sum(d_first * norm_one, axis=0)
    grad_shift_one = jnp.sum(d_first, axis=0)
    d_resid = norm_back(d_first, norm_one, scale_one, gain_one)
    d_attended = d_resid.astype(BF)
    grad_w_output = dot_tn(mixed, d_attended)
    grad_b_output = jnp.sum(d_attended.astype(F32), axis=0)
    d_mixed = dot_nt(d_attended, w_output).astype(BF)

    def owned(grad):
        return grad.astype(BF).reshape(dp_size, seq_size, grad.shape[0] // owners, width)

    tail_grads = [owned(grad_w_output)]
    tail_grads += [owned(grad_w_inner[:, i * width : (i + 1) * width]) for i in range(fan)]
    tail_sum = scatter_sum(jnp.concatenate(tail_grads + [owned(grad_w_outer)], axis=2))

    d_states = mixer.query_states(qkv, d_mixed, mixed_full, den, bias_row, cos, sin)
    later = outside_sum(d_states, False)
    d_query, d_key, d_value = mixer.mix_back(qkv, d_mixed, mixed_full, den, bias_row, low, up, cos, sin, past, later)
    d_three = (d_query, d_key, d_value)
    grad_w = [dot_tn(x_low, d) for d in d_three]
    grad_b = [jnp.sum(d.astype(F32), axis=0) for d in d_three]
    d_tokens = d_resid
    for i, d in enumerate(d_three):
        d_tokens = d_tokens + dot_nt(d, w_qkv[:, i * width : (i + 1) * width])

    vec_grads = grad_b + [grad_b_output, grad_gain_one, grad_shift_one, grad_b_outer, grad_gain_two, grad_shift_two]
    vec_rows = jnp.concatenate(
        [g.reshape(owners, share) for g in vec_grads] + [grad_b_inner.reshape(owners, hidden_width // owners)], axis=1
    )
    vec_rows = jnp.pad(vec_rows[:, None, :], ((0, 0), (0, 7), (0, vector_fill)))
    vec_rows = vec_rows.reshape(dp_size, seq_size, 8, width).astype(BF)
    head_sum_rows = scatter_sum(jnp.concatenate([vec_rows] + [owned(g) for g in grad_w], axis=2))

    vec_out = head_sum_rows[0]
    out_vec = [vec_out[i * share : (i + 1) * share] for i in range(9)]
    out_b_inner = vec_out[9 * share : 9 * share + hidden_width // owners]
    out_w = [head_sum_rows[8 + i * share : 8 + (i + 1) * share] for i in range(3)]
    out_w_output = tail_sum[:share]
    out_w_inner = jnp.concatenate([tail_sum[(1 + i) * share : (2 + i) * share] for i in range(fan)], axis=1)
    out_w_outer = tail_sum[(1 + fan) * share :]
    return (
        layer_out.reshape(tokens.shape),
        d_tokens.reshape(tokens.shape),
        out_w[0],
        out_vec[0],
        out_w[1],
        out_vec[1],
        out_w[2],
        out_vec[2],
        out_w_output,
        out_vec[3],
        out_vec[4],
        out_vec[5],
        out_w_inner,
        out_b_inner,
        out_w_outer,
        out_vec[6],
        out_vec[7],
        out_vec[8],
    )


def solution(mesh):
    rows = P(("dp", "seq"), None)
    vector = P(("dp", "seq"))
    act = P(None, "dp", "seq", None)
    layer = (rows, vector) * 4 + (vector, vector) + (rows, vector) * 2 + (vector, vector)
    return jax.shard_map(
        per_device,
        mesh=mesh,
        in_specs=(act, P(None, "dp")) + layer + (act,),
        out_specs=(act, act) + layer,
        check_vma=False,
    )
```

```python
import math

import jax
import jax.numpy as jnp
from jax import lax
from jax.experimental import pallas as pl
from jax.experimental.pallas import tpu as pltpu
from jax.sharding import PartitionSpec as P

H = 12
HD = 64
LANES = 128
NORM_EPS = 1e-05
HALF_TURN = math.pi / 2
STATE_ROWS = 72
GELU_A = 0.7978845608028654
GELU_B = 0.044715
BF = jnp.bfloat16
F32 = jnp.float32


def dot_nn(a, b):
    return lax.dot_general(a, b, (((1,), (0,)), ((), ())), preferred_element_type=F32)


def dot_nt(a, b):
    return lax.dot_general(a, b, (((1,), (1,)), ((), ())), preferred_element_type=F32)


def dot_tn(a, b):
    return lax.dot_general(a, b, (((0,), (0,)), ((), ())), preferred_element_type=F32)


def lane_first(shape):
    return lax.broadcasted_iota(jnp.int32, shape, 1) < HD


def pair_ones():
    row = lax.broadcasted_iota(jnp.int32, (LANES, LANES), 0) < HD
    col = lax.broadcasted_iota(jnp.int32, (LANES, LANES), 1) < HD
    return (row == col).astype(F32)


def head_sum(values, ones_low):
    high = values.astype(BF)
    rest = (values - high.astype(F32)).astype(BF)
    return dot_nn(jnp.concatenate([high, rest], axis=1), jnp.concatenate([ones_low, ones_low], axis=0))


def spread_state(packed):
    first = lane_first((HD, LANES))
    zero = jnp.zeros_like(packed)
    return jnp.concatenate(
        [jnp.where(first, packed, zero), jnp.where(first, zero, packed)], axis=0
    ).astype(BF)


def pack_state(full, row):
    first = lane_first((HD, LANES))
    packed = jnp.where(first, full[:HD], full[HD:])
    tail = jnp.concatenate([row, jnp.zeros((STATE_ROWS - HD - 1, LANES), F32)], axis=0)
    return jnp.concatenate([packed, tail], axis=0)


QUERY, KEY, VALUE = (slice(i * LANES, (i + 1) * LANES) for i in range(3))


def weave(parts):
    pairs = parts[0].shape[-1] // LANES
    split = [part.reshape(part.shape[:-1] + (pairs, 1, LANES)) for part in parts]
    return jnp.concatenate(split, axis=-2).reshape(parts[0].shape[:-1] + (3 * pairs * LANES,))


def unweave(woven):
    split = woven.reshape(woven.shape[:-1] + (-1, 3, LANES))
    return [split[..., i, :].reshape(woven.shape[:-1] + (-1,)) for i in range(3)]


def key_state_kernel(qkv_ref, cos_ref, sin_ref, out_ref):
    keys = jnp.maximum(qkv_ref[:, KEY], 0)
    vals = qkv_ref[:, VALUE].astype(F32)
    cos, sin = cos_ref[...], sin_ref[...]
    both = jnp.concatenate([(vals * cos).astype(BF), (vals * sin).astype(BF)], axis=1)
    full = dot_tn(keys, both)
    keys32 = keys.astype(F32)
    row_cos = jnp.sum(keys32 * cos, axis=0, keepdims=True)
    row_sin = jnp.sum(keys32 * sin, axis=0, keepdims=True)
    out_ref[0, 0] = pack_state(full[:, :LANES], row_cos).astype(BF)
    out_ref[0, 1] = pack_state(full[:, LANES:], row_sin).astype(BF)


def tile_rows(rows):
    return min(256, rows)


def mix_kernel(qkv_ref, b_ref, w_ref, cos_ref, sin_ref, st_ref, mixed_ref, out_ref, den_ref):
    rows = qkv_ref.shape[0]
    tile = tile_rows(rows)
    ones_pair = pair_ones().astype(BF)
    keys = jnp.maximum(qkv_ref[:, KEY], 0)
    vals = jnp.concatenate([qkv_ref[:, VALUE], jnp.ones((rows, LANES), BF)], axis=1)
    states = jnp.concatenate(
        [spread_state(st_ref[0, 0, :HD]), spread_state(st_ref[0, 1, :HD])], axis=1
    )
    row_cos, row_sin = st_ref[0, 0, HD : HD + 1], st_ref[0, 1, HD : HD + 1]
    first = lane_first((tile, LANES))
    for step in range(rows // tile):
        at = slice(step * tile, (step + 1) * tile)
        seen = (step + 1) * tile
        query = jnp.maximum(qkv_ref[at, QUERY], 0)
        cos, sin = cos_ref[at], sin_ref[at]
        zero = jnp.zeros_like(query)
        weight = w_ref[0, at, :seen]
        heads = []
        for own in (jnp.where(first, query, zero), jnp.where(first, zero, query)):
            scores = dot_nt(own, keys[:seen]) * weight
            heads.append(dot_nn(scores.astype(BF), vals[:seen]))
        num = jnp.where(first, heads[0][:, :LANES], heads[1][:, :LANES])
        den = jnp.where(first, heads[0][:, LANES:], heads[1][:, LANES:])
        past = dot_nn(query, states)
        num = num + cos * past[:, :LANES] + sin * past[:, LANES:]
        den = den + head_sum(query.astype(F32) * (cos * row_cos + sin * row_sin), ones_pair)
        out = (num + den * b_ref[...]) / jnp.maximum(den, 1.0)
        mixed_ref[at] = out.astype(BF)
        out_ref[at] = out
        den_ref[at] = den


def mix_grads(d_out, out, den, bias, ones_pair):
    inverse = 1.0 / jnp.maximum(den, 1.0)
    d_num = (d_out.astype(F32) * inverse).astype(BF)
    gate = jnp.where(den > 1.0, 1.0, jnp.where(den == 1.0, 0.5, 0.0))
    return d_num, head_sum(d_num.astype(F32) * (bias - out * gate), ones_pair)


def query_state_kernel(qkv_ref, d_ref, out_ref, den_ref, b_ref, cos_ref, sin_ref, st_ref):
    ones_pair = pair_ones().astype(BF)
    query = jnp.maximum(qkv_ref[:, QUERY], 0)
    cos, sin = cos_ref[...], sin_ref[...]
    d_num, d_den = mix_grads(d_ref[...], out_ref[...], den_ref[...], b_ref[...], ones_pair)
    d_num32 = d_num.astype(F32)
    both = jnp.concatenate([(d_num32 * cos).astype(BF), (d_num32 * sin).astype(BF)], axis=1)
    full = dot_tn(query, both)
    part = query.astype(F32) * d_den
    st_ref[0, 0] = pack_state(full[:, :LANES], jnp.sum(part * cos, axis=0, keepdims=True)).astype(BF)
    st_ref[0, 1] = pack_state(full[:, LANES:], jnp.sum(part * sin, axis=0, keepdims=True)).astype(BF)


def mix_back_kernel(
    qkv_ref, d_ref, out_ref, den_ref, b_ref, low_ref, up_ref, cos_ref, sin_ref, past_ref, next_ref,
    grad_ref, sum_ref,
):
    rows = qkv_ref.shape[0]
    tile = tile_rows(rows)
    ones_pair = pair_ones().astype(BF)
    first = lane_first((rows, LANES))
    lane = lax.broadcasted_iota(jnp.int32, (rows, LANES), 1)
    query = jnp.maximum(qkv_ref[:, QUERY], 0)
    keys = jnp.maximum(qkv_ref[:, KEY], 0)
    vals = qkv_ref[:, VALUE]
    cos, sin = cos_ref[...], sin_ref[...]
    d_num, d_den = mix_grads(d_ref[...], out_ref[...], den_ref[...], b_ref[...], ones_pair)
    high = d_den.astype(BF)
    rest = (d_den - high.astype(F32)).astype(BF)
    zero = jnp.zeros((rows, LANES), BF)
    spot = lane % HD
    marks = jnp.where(spot == 0, high, jnp.where(spot == 1, rest, zero))
    vals_one = jnp.concatenate([vals, jnp.ones((rows, LANES), BF)], axis=1)

    past = [spread_state(past_ref[0, i, :HD]) for i in range(2)]
    past_row = [past_ref[0, i, HD : HD + 1] for i in range(2)]
    d_query = cos * dot_nt(d_num, past[0]) + sin * dot_nt(d_num, past[1])
    d_query = d_query + d_den * (cos * past_row[0] + sin * past_row[1])
    later = [spread_state(next_ref[0, i, :HD]) for i in range(2)]
    later_row = [next_ref[0, i, HD : HD + 1] for i in range(2)]
    d_keys = cos * (dot_nt(vals, later[0]) + later_row[0]) + sin * (dot_nt(vals, later[1]) + later_row[1])
    from_keys = dot_nn(keys, jnp.concatenate(later, axis=1))
    d_vals = cos * from_keys[:, :LANES] + sin * from_keys[:, LANES:]

    own_query = (jnp.where(first, query, zero), jnp.where(first, zero, query))
    own_d = tuple(
        jnp.concatenate([jnp.where(pick, d_num, zero), jnp.where(pick, marks, zero)], axis=1)
        for pick in (first, jnp.logical_not(first))
    )
    sums = [jnp.zeros((1, LANES), F32)] * 3
    for step in range(rows // tile):
        at = slice(step * tile, (step + 1) * tile)
        seen = (step + 1) * tile
        some = first[at]
        parts = []
        for one in range(2):
            d_scores = dot_nt(own_d[one][at], vals_one[:seen]) * low_ref[0, at, :seen]
            parts.append(dot_nn(d_scores.astype(BF), keys[:seen]))
        total = d_query[at] + jnp.where(some, parts[0], parts[1])
        grads = [jnp.where(query[at] > 0, total, 0.0).astype(BF)]
        onward = slice(step * tile, rows)
        weight = up_ref[0, at, onward]
        key_parts, val_parts = [], []
        for one in range(2):
            scores = dot_nt(keys[at], own_query[one][onward]) * weight
            val_parts.append(dot_nn(scores.astype(BF), d_num[onward]))
            d_scores = dot_nt(vals_one[at], own_d[one][onward]) * weight
            key_parts.append(dot_nn(d_scores.astype(BF), query[onward]))
        total = d_keys[at] + jnp.where(some, key_parts[0], key_parts[1])
        grads.append(jnp.where(keys[at] > 0, total, 0.0).astype(BF))
        grads.append((d_vals[at] + jnp.where(some, val_parts[0], val_parts[1])).astype(BF))
        for lanes, grad in zip((QUERY, KEY, VALUE), grads):
            grad_ref[at, lanes] = grad
        sums = [total + jnp.sum(grad.astype(F32), axis=0, keepdims=True) for total, grad in zip(sums, grads)]
    sum_ref[0] = jnp.concatenate(sums, axis=1)


class Mixer:
    def __init__(self, count, rows, width, first_pair):
        self.count, self.rows, self.width = count, rows, width
        self.pairs, self.first_pair = width // LANES, first_pair

    def wide(self):
        return pl.BlockSpec((self.rows, LANES), lambda m, p: (m, p))

    def wide_of_all(self):
        start = self.first_pair
        return pl.BlockSpec((self.rows, LANES), lambda m, p: (m, start + p))

    def woven(self):
        return pl.BlockSpec((self.rows, 3 * LANES), lambda m, p: (m, p))

    def angle(self):
        return pl.BlockSpec((self.rows, LANES), lambda m, p: (m, 0))

    def bias(self):
        start = self.first_pair
        return pl.BlockSpec((1, LANES), lambda m, p: (0, start + p))

    def row(self):
        return pl.BlockSpec((1, 1, 3 * LANES), lambda m, p: (m, 0, p))

    def state(self):
        return pl.BlockSpec((1, 2, STATE_ROWS, LANES), lambda m, p: (m, 0, 0, p))

    def square(self):
        return pl.BlockSpec((1, self.rows, self.rows), lambda m, p: (m, 0, 0))

    def state_shape(self):
        return jax.ShapeDtypeStruct((self.count, 2, STATE_ROWS, self.width), BF)

    def flat_shape(self, dtype):
        return jax.ShapeDtypeStruct((self.count * self.rows, self.width), dtype)

    def call(self, kernel, in_specs, out_specs, out_shape, flops):
        return pl.pallas_call(
            kernel,
            grid=(self.count, self.pairs),
            in_specs=in_specs,
            out_specs=out_specs,
            out_shape=out_shape,
            cost_estimate=pl.CostEstimate(
                flops=flops * self.count * self.pairs, bytes_accessed=1 << 23, transcendentals=0
            ),
        )

    def key_states(self, qkv, cos, sin):
        flops = 4 * self.rows * LANES * LANES
        return self.call(
            key_state_kernel,
            [self.woven(), self.angle(), self.angle()],
            self.state(),
            self.state_shape(),
            flops,
        )(qkv, cos, sin)

    def mix(self, qkv, bias, low, cos, sin, past):
        flops = 12 * self.rows * self.rows * LANES
        return self.call(
            mix_kernel,
            [self.woven(), self.bias(), self.square(), self.angle(), self.angle(), self.state()],
            [self.wide()] * 3,
            [self.flat_shape(BF), self.flat_shape(F32), self.flat_shape(F32)],
            flops,
        )(qkv, bias, low, cos, sin, past)

    def query_states(self, qkv, d_mixed, out, den, bias, cos, sin):
        flops = 4 * self.rows * LANES * LANES
        return self.call(
            query_state_kernel,
            [self.woven(), self.wide_of_all()] + [self.wide()] * 2 + [self.bias()] + [self.angle()] * 2,
            self.state(),
            self.state_shape(),
            flops,
        )(qkv, d_mixed, out, den, bias, cos, sin)

    def mix_back(self, qkv, d_mixed, out, den, bias, low, up, cos, sin, past, later):
        flops = 30 * self.rows * self.rows * LANES
        return self.call(
            mix_back_kernel,
            [self.woven(), self.wide_of_all()]
            + [self.wide()] * 2
            + [self.bias()]
            + [self.square()] * 2
            + [self.angle()] * 2
            + [self.state()] * 2,
            [self.woven(), self.row()],
            [
                jax.ShapeDtypeStruct((self.count * self.rows, 3 * self.width), BF),
                jax.ShapeDtypeStruct((self.count, 1, 3 * self.width), F32),
            ],
            flops,
        )(qkv, d_mixed, out, den, bias, low, up, cos, sin, past, later)


def outside_sum(states, forward, between=None):
    size = lax.axis_size("seq")

    def shift(values, distance):
        if forward:
            pairs = [(i, i + distance) for i in range(size - distance)]
        else:
            pairs = [(i + distance, i) for i in range(size - distance)]
        return [lax.ppermute(value, "seq", pairs) for value in values]

    moved = shift(states, 1)
    if between is not None:
        moved = between(moved)
    totals = [value.astype(F32) for value in moved]
    reach = 1
    while reach + 1 < size:
        if 2 * reach + 1 > size - 1:
            raise NotImplementedError
        blocks = [(state.astype(F32) + total).astype(BF) for state, total in zip(states, totals)]
        totals = [total + got.astype(F32) for total, got in zip(totals, shift(blocks, reach + 1))]
        reach = 2 * reach + 1
    return totals


def swap(values, bit):
    size = lax.axis_size("dp")
    return lax.ppermute(values, "dp", [(i, i ^ (1 << bit)) for i in range(size)])


def own_place(name):
    if name == "seq":
        return lax.axis_index("seq")
    return (lax.axis_index("dp") >> name) & 1


def picked(array, names, picks, lanes=slice(None)):
    first, last, _ = lanes.indices(array.shape[-1])
    starts, sizes = [0] * array.ndim, list(array.shape)
    for name, at in picks.items():
        if name in names:
            axis = names.index(name)
            starts[axis], sizes[axis] = at, 1
    starts[-1], sizes[-1] = first, last - first
    left = [size for name, size in zip(names, sizes) if name not in picks]
    return lax.dynamic_slice(array, starts, sizes).reshape(left + sizes[len(names) :]).astype(F32)


class Pair:
    def __init__(self, grad):
        dp_size, seq_size = lax.axis_size("dp"), lax.axis_size("seq")
        bits = dp_size.bit_length() - 1
        rows, width = grad.shape
        self.names = list(range(bits - 1, -1, -1)) + ["seq"]
        self.kept = grad.reshape((2,) * bits + (seq_size, rows // (dp_size * seq_size), width))
        self.fresh = [swap(self.kept, 0)]

    def piece(self, picks, lanes=slice(None)):
        picks = {**picks, 0: own_place(0)}
        return sum(picked(array, self.names, picks, lanes) for array in (self.kept, self.fresh[0]))


class Beside:
    def __init__(self, pairs):
        self.pairs = pairs

    def piece(self, picks, lanes):
        parts, first = [], 0
        for pair in self.pairs:
            last = first + pair.kept.shape[-1]
            low, high = max(lanes.start, first), min(lanes.stop, last)
            if low < high:
                parts.append(pair.piece(picks, slice(low - first, high - first)))
            first = last
        return parts[0] if len(parts) == 1 else jnp.concatenate(parts, axis=-1)


class Columns:
    def __init__(self, source, first, last):
        self.source, self.lanes = source, slice(first, last)

    def piece(self, picks):
        return self.source.piece(picks, self.lanes)


class Chain:
    def __init__(self, sources, left):
        self.sources, self.left = sources, left
        self.arrived, self.names, self.picks = [], [], {}
        self.fresh = []

    def piece(self, picks):
        picks = {**self.picks, **picks}
        parts = [source.piece(picks) for source in self.sources]
        total = parts[0] if len(parts) == 1 else jnp.concatenate(parts, axis=-1)
        for array, names in zip(self.arrived + self.fresh, self.names):
            total = total + picked(array, names, picks)
        return total

    def step(self, name):
        mine = own_place(name)
        rest = [n for n in self.left if n != name]
        if name == "seq":
            size = lax.axis_size("seq")
            got = []
            for distance in range(1, size):
                sent = self.piece({"seq": (mine + distance) % size}).astype(BF)
                got.append(lax.ppermute(sent, "seq", [(i, (i + distance) % size) for i in range(size)]))
        else:
            got = [swap(self.piece({name: 1 - mine}).astype(BF), name)]
        self.arrived = self.arrived + self.fresh
        self.fresh = got
        self.names = self.names + [rest] * len(got)
        self.picks = {**self.picks, name: mine}
        self.left = rest
        return self

    def steps(self, names):
        for name in names:
            self.step(name)
        return self


class Ways:
    def __init__(self, source, width, left, along_x, along_y):
        self.along = (along_x, along_y)
        middle = width // 2
        self.chains = [Chain([Columns(source, 0, middle)], left), Chain([Columns(source, middle, width)], left)]

    def first(self):
        for chain, names in zip(self.chains, self.along):
            chain.steps(names)
        return self

    def second(self):
        for chain, names in zip(self.chains, self.along[::-1]):
            chain.steps(names)
        return self

    def join(self):
        return Chain(self.chains, ["seq"]).step("seq")


class Spread:
    def __init__(self, block, have=()):
        self.block, self.have, self.pending, self.fresh = block, list(have), None, []

    def joined(self):
        if self.pending is None:
            return self.block
        name, axis = self.pending
        mine = own_place(name)
        pieces = [self.block] + self.fresh
        count = len(pieces)
        value = None
        for place in range(count):
            turned = jnp.stack([pieces[(place - at) % count] for at in range(count)], axis=axis)
            value = turned if value is None else jnp.where(mine == place, turned, value)
        self.block, self.pending, self.fresh = value, None, []
        return self.block

    def step(self, name):
        block = self.joined()
        axis = len([n for n in self.have if n != "seq" and (name == "seq" or n > name)])
        if name == "seq":
            size = lax.axis_size("seq")
            shifts = [[(i, (i + distance) % size) for i in range(size)] for distance in range(1, size)]
            self.fresh = [lax.ppermute(block, "seq", pairs) for pairs in shifts]
        else:
            self.fresh = [swap(block, name)]
        self.pending = (name, axis)
        self.have.insert(axis, name)
        return self

    def steps(self, names):
        for name in names:
            self.step(name)
        return self

    def columns(self, first, last):
        return Spread(self.joined()[..., first:last], self.have)

    def whole(self):
        block = self.joined()
        return block.reshape(-1, block.shape[-1])


class Vectors:
    def __init__(self, values):
        self.values, self.fresh = values, []

    def total(self):
        for got in self.fresh:
            self.values = self.values + got
        self.fresh = []
        return self.values

    def step(self, name):
        values = self.total()
        if name == "seq":
            size = lax.axis_size("seq")
            for distance in range(1, size):
                self.fresh.append(lax.ppermute(values, "seq", [(i, (i + distance) % size) for i in range(size)]))
        else:
            self.fresh = [swap(values, name)]

    def steps(self, names):
        for name in names:
            self.step(name)


def tie(values, items):
    values, held = lax.optimization_barrier((values, [item.fresh for item in items]))
    for item, fresh in zip(items, held):
        item.fresh = fresh
    return values


def norm_stats(values):
    center = values - jnp.mean(values, axis=-1, keepdims=True)
    spread = jnp.mean(center * center, axis=-1, keepdims=True)
    scale = lax.rsqrt(spread + NORM_EPS)
    return center * scale, scale


def norm_back(grad, normed, scale, gain):
    inner = grad * gain
    return scale * (
        inner
        - jnp.mean(inner, axis=-1, keepdims=True)
        - normed * jnp.mean(inner * normed, axis=-1, keepdims=True)
    )


def per_device(
    tokens,
    seq_lengths,
    query_weight,
    query_bias,
    key_weight,
    key_bias,
    value_weight,
    value_bias,
    output_weight,
    output_bias,
    gain_first,
    shift_first,
    inner_weight,
    inner_bias,
    outer_weight,
    outer_bias,
    gain_second,
    shift_second,
    cotangent,
):
    dp_size, seq_size = lax.axis_size("dp"), lax.axis_size("seq")
    owners = dp_size * seq_size
    micro_count, seqs_here, shard_rows, width = tokens.shape
    count = micro_count * seqs_here
    total = count * shard_rows
    share = query_weight.shape[0]
    hidden_width = inner_weight.shape[1]
    fan = hidden_width // width
    seq_place = lax.axis_index("seq")
    bits = dp_size.bit_length() - 1
    half_bits = (bits - 1) // 2
    along_x, along_y = list(range(1, 1 + half_bits)), list(range(1 + half_bits, bits))
    chip_axes = list(range(bits - 1, 0, -1)) + ["seq"]
    half = width // 2
    mixers = [Mixer(count, shard_rows, half, i * half // LANES) for i in range(2)]

    vectors = [query_bias, key_bias, value_bias, output_bias, gain_first, shift_first, outer_bias, gain_second, shift_second]
    columns = jnp.concatenate([v[None, :] for v in vectors] + [inner_bias.reshape(fan, share)], axis=0)
    columns = jnp.pad(columns, ((0, LANES - 9 - fan), (0, 0))).T
    head_rows = jnp.concatenate([columns, weave([query_weight, key_weight, value_weight])], axis=1)
    head_rows, inner_shard = lax.optimization_barrier((head_rows, inner_weight))
    head = Spread(head_rows).step("seq")
    tail_rows = jnp.concatenate(
        [output_weight] + [inner_shard[:, i * width : (i + 1) * width] for i in range(fan)] + [outer_weight], axis=0
    )
    tail_all = lax.all_gather(tail_rows, ("dp", "seq"), axis=0)
    middle = LANES + 3 * half
    sides = [head.columns(0, middle), head.columns(middle, LANES + 3 * width)]
    sides[0].steps(along_x + along_y + [0])
    sides[1].steps(along_y + along_x + [0])
    w_halves = [side.whole() for side in sides]

    vec = w_halves[0][:, :LANES].T.astype(F32)
    w_halves[0] = w_halves[0][:, LANES:]
    (b_query, b_key, b_value, b_output, gain_one, shift_one, b_outer, gain_two, shift_two) = (vec[i] for i in range(9))
    b_inner = vec[9 : 9 + fan].reshape(fan, owners, share).transpose(1, 0, 2).reshape(hidden_width)
    b_qkv = weave([b_query, b_key, jnp.zeros((width,), F32)])
    bias_row = b_value[None, :]

    limit = seq_lengths.reshape(count).astype(F32)
    places = (seq_place * shard_rows + jnp.arange(shard_rows)).astype(F32)
    angle = HALF_TURN * places[None, :] / limit[:, None]
    live = (places[None, :] < limit[:, None]).astype(F32)
    cos, sin = jnp.cos(angle) * live, jnp.sin(angle) * live
    square = cos[:, :, None] * cos[:, None, :] + sin[:, :, None] * sin[:, None, :]
    causal = jnp.tril(jnp.ones((shard_rows, shard_rows), F32))
    low, up = square * causal, square * causal.T
    cos = jnp.broadcast_to(cos.reshape(total, 1), (total, LANES))
    sin = jnp.broadcast_to(sin.reshape(total, 1), (total, LANES))

    x_low = tokens.reshape(total, width)
    qkv = [(dot_nn(x_low, w) + b_qkv[i * 3 * half : (i + 1) * 3 * half]).astype(BF) for i, w in enumerate(w_halves)]
    states = [mixer.key_states(woven, cos, sin) for mixer, woven in zip(mixers, qkv)]
    past = [outside_sum([state], True)[0] for state in states]
    front = [mixers[i].mix(qkv[i], bias_row, low, cos, sin, past[i]) for i in range(2)]
    mixed = jnp.concatenate([f[0] for f in front], axis=1)
    w_output = tail_all[:, :share].reshape(width, width)
    w_inner = jnp.concatenate(
        [tail_all[:, (1 + i) * share : (2 + i) * share].reshape(width, width) for i in range(fan)], axis=1
    )
    w_outer = tail_all[:, (1 + fan) * share :].reshape(hidden_width, width)

    resid_one = x_low.astype(F32) + (dot_nn(mixed, w_output) + b_output)
    norm_one, scale_one = norm_stats(resid_one)
    first = norm_one * gain_one + shift_one
    first_low = first.astype(BF)
    inner = dot_nn(first_low, w_inner) + b_inner
    bent = jnp.tanh(GELU_A * (inner + GELU_B * inner * inner * inner))
    hidden = (0.5 * inner * (1.0 + bent)).astype(BF)
    outer = dot_nn(hidden, w_outer) + b_outer
    norm_two, scale_two = norm_stats(first + outer)
    layer_out = (norm_two * gain_two + shift_two).astype(BF)

    grad_final = cotangent.reshape(total, width).astype(F32)
    grad_gain_two = jnp.sum(grad_final * norm_two, axis=0)
    grad_shift_two = jnp.sum(grad_final, axis=0)
    d_second = norm_back(grad_final, norm_two, scale_two, gain_two)
    d_outer = d_second.astype(BF)
    grad_b_outer = jnp.sum(d_outer.astype(F32), axis=0)
    pair_outer = Pair(dot_tn(hidden, d_outer).astype(BF))
    d_hidden = dot_nt(d_outer, w_outer)
    slope = 0.5 * (1.0 + bent) + 0.5 * inner * (1.0 - bent * bent) * GELU_A * (1.0 + 3.0 * GELU_B * inner * inner)
    d_inner = (d_hidden * slope).astype(BF)
    d_inner = tie(d_inner, [pair_outer])
    outer_ways = Ways(pair_outer, width, chip_axes, along_x, along_y).first()
    grad_b_inner = jnp.sum(d_inner.astype(F32), axis=0)
    d_first = d_second + dot_nt(d_inner, w_inner)
    d_first = tie(d_first, outer_ways.chains)
    outer_ways.second()
    grad_gain_one = jnp.sum(d_first * norm_one, axis=0)
    grad_shift_one = jnp.sum(d_first, axis=0)
    d_resid = norm_back(d_first, norm_one, scale_one, gain_one)
    d_attended = d_resid.astype(BF)
    grad_b_output = jnp.sum(d_attended.astype(F32), axis=0)
    d_mixed = dot_nt(d_attended, w_output).astype(BF)

    d_states = [
        mixers[i].query_states(qkv[i], d_mixed, front[i][1], front[i][2], bias_row, cos, sin) for i in range(2)
    ]
    d_states, d_inner_late = tie((d_states, d_inner), outer_ways.chains)
    late = {}

    def between(moved):
        inner_grad = dot_tn(first_low, d_inner_late).astype(BF)
        moved, inner_grad, d_late = lax.optimization_barrier((moved, inner_grad, d_attended))
        late["inner"], late["output"] = inner_grad, dot_tn(mixed, d_late).astype(BF)
        return moved

    later = outside_sum(d_states, False, between)
    pair_inner, pair_output = Pair(late["inner"]), Pair(late["output"])
    d_mixed, later = tie((d_mixed, later), [pair_inner, pair_output] + outer_ways.chains)
    outer_sum = outer_ways.join()
    inner_ways = Ways(Beside([pair_inner, pair_output]), hidden_width + width, chip_axes, along_x, along_y).first()
    mix_back_of = [
        lambda d_all, i=i: mixers[i].mix_back(
            qkv[i], d_all, front[i][1], front[i][2], bias_row, low, up, cos, sin, past[i], later[i]
        )
        for i in range(2)
    ]
    d_one, sum_one = mix_back_of[0](d_mixed)
    d_one = tie(d_one, [outer_sum] + inner_ways.chains)
    inner_ways.second()
    grad_one = dot_tn(x_low, d_one).astype(BF)
    d_mixed, grad_one = lax.optimization_barrier((d_mixed, grad_one))
    pair_one = Pair(grad_one)
    d_two, sum_two = mix_back_of[1](d_mixed)
    d_two = tie(d_two, inner_ways.chains + [pair_one])
    one = Chain([pair_one], chip_axes).steps(along_x)
    inner_sum = inner_ways.join()
    grad_two = dot_tn(x_low, d_two).astype(BF)
    pair_two = Pair(grad_two)
    d_one, d_two = lax.optimization_barrier((d_one, d_two, grad_two))[:2]
    d_tokens = d_resid + dot_nt(d_one, w_halves[0]) + dot_nt(d_two, w_halves[1])
    sums = [jnp.sum(total, axis=(0, 1)) for total in (sum_one, sum_two)]
    rows = [jnp.concatenate([unweave(total)[i] for total in sums]) for i in range(3)]
    rows += [grad_b_output, grad_gain_one, grad_shift_one, grad_b_outer, grad_gain_two, grad_shift_two]
    rows = [row[None, :] for row in rows] + [grad_b_inner[None, i * width : (i + 1) * width] for i in range(fan)]
    vectors = Vectors(jnp.concatenate(rows + [jnp.zeros((7 - (8 + fan) % 8, width), F32)], axis=0))
    vectors.step(0)
    tie((), [one, pair_two, vectors])
    two = Chain([pair_two], chip_axes).steps(along_x)
    one.steps(along_y)
    vectors.steps(along_x)
    tie((), [one, two, vectors])
    two.steps(along_y)
    one.step("seq")
    vectors.steps(along_y)
    tie((), [inner_sum, one, two, vectors])
    two.step("seq")
    vectors.step("seq")

    place = lax.axis_index("dp") * seq_size + seq_place
    table = vectors.total()
    own_columns = lax.dynamic_slice(table, (0, place * share), (9, share))
    out_vec = [own_columns[i] for i in range(9)]
    inner_share = hidden_width // owners
    at = place * inner_share
    out_b_inner = lax.dynamic_slice(table, (9 + at // width, at % width), (1, inner_share))[0]
    out_w_outer = outer_sum.piece({})
    inner_and_output = inner_sum.piece({})
    out_w_inner, out_w_output = inner_and_output[:, :hidden_width], inner_and_output[:, hidden_width:]
    out_w = unweave(jnp.concatenate([one.piece({}), two.piece({})], axis=1))
    return (
        layer_out.reshape(tokens.shape),
        d_tokens.reshape(tokens.shape),
        out_w[0],
        out_vec[0],
        out_w[1],
        out_vec[1],
        out_w[2],
        out_vec[2],
        out_w_output,
        out_vec[3],
        out_vec[4],
        out_vec[5],
        out_w_inner,
        out_b_inner,
        out_w_outer,
        out_vec[6],
        out_vec[7],
        out_vec[8],
    )


def solution(mesh):
    rows = P(("dp", "seq"), None)
    vector = P(("dp", "seq"))
    act = P(None, "dp", "seq", None)
    layer = (rows, vector) * 4 + (vector, vector) + (rows, vector) * 2 + (vector, vector)
    return jax.shard_map(
        per_device,
        mesh=mesh,
        in_specs=(act, P(None, "dp")) + layer + (act,),
        out_specs=(act, act) + layer,
        check_vma=False,
    )
```
